32 devices in a mesh: dp: 8 (over y, x, core), ctx: 4 (over z).
Axes of the slice: x: 2, y: 2, z: 4, core: 2. Of those that a mesh axis runs over, the one named last changes fastest.
Arguments:
- queries: bfloat16 [4096, 2048], P(('dp', 'ctx')), may hold values from -120 to 120
- keys: bfloat16 [4096, 512], P(('dp', 'ctx')), may hold values from -5.5 to 5.5
- values: bfloat16 [4096, 512], P(('dp', 'ctx')), may hold values from -6 to 6
- output_gradient: bfloat16 [4096, 2048], P(('dp', 'ctx')), may hold values from -6 to 6
- doc_blocks: int32 [16], P('dp'), may hold values from 1 to 3, 32 in all
- doc_pad: int32 [16], P('dp'), may hold values from 0 to 127
Outputs:
- attn_out: bfloat16 [4096, 2048], P(('dp', 'ctx'))
- grad_queries: bfloat16 [4096, 2048], P(('dp', 'ctx'))
- grad_keys: bfloat16 [4096, 512], P(('dp', 'ctx'))
- grad_values: bfloat16 [4096, 512], P(('dp', 'ctx'))
The draws below stay inside these ranges and needn't reach their ends.
All inputs are finite; a program needn't handle non-finite values. No bound on the sum of `doc_blocks` on one device may be relied on, other than what follows from the above.
Results may differ from the reference program's by a relative error of at most 0.02.
Values may be sent and summed in bfloat16 or wider, within the bound.
No kernel may reach another device: no remote copies, remote signals or barrier semaphores. Data moves between devices by JAX's collectives and lax.ppermute only.
A program may use at most 64 MiB of HBM per device.

```python
import math
import jax
import jax.numpy as jnp
import numpy as np
from jax import lax

QUERY_HEADS = 16
KEY_VALUE_HEADS = 4
HEAD_SIZE = 128
DEVICE_TOKENS = 128
MOST_DOC_BLOCKS = 3
DOCS = 16
BLOCK_TOTAL = 32
TOKEN_SLOTS = 4096


def draw_keys(key, part):
    reshaped_tensor = jnp.clip(jax.random.normal(jax.random.fold_in(key, 11), (TOKEN_SLOTS, KEY_VALUE_HEADS * HEAD_SIZE), jnp.float32), -5.0, 5.0)
    return reshaped_tensor.astype(jnp.bfloat16)


def draw_queries(key, part):
    base_queries = jnp.clip(jax.random.normal(jax.random.fold_in(key, 19), (TOKEN_SLOTS, QUERY_HEADS * HEAD_SIZE), jnp.float32), -5.0, 5.0)
    return base_queries.astype(jnp.bfloat16)


def with_ends(result, own_key, smallest, high):
    index_at = [jax.random.randint(jax.random.fold_in(own_key, axis), (), 0, length) for axis, length in enumerate(result.shape)]
    widest = result.shape.index(max(result.shape))
    beside = index_at[:widest] + [(index_at[widest] + 1) % result.shape[widest]] + index_at[widest + 1:]
    return result.at[tuple(index_at)].set(smallest).at[tuple(beside)].set(high)


def shard_levels(stream_key, dims, split, low, high):
    loudness, own = 1.0, jax.random.fold_in(stream_key, 6)
    for dim, shards_of in split:
        draws = jnp.exp(jax.random.uniform(jax.random.fold_in(own, dim), (shards_of,), jnp.float32, low / len(split), high / len(split)))
        loudness = loudness * jnp.repeat(draws, dims[dim] // shards_of).reshape([-1 if axis == dim else 1 for axis in range(len(dims))])
    return loudness


def split_up(number_of, total, most, slope):
    portions = [(1 << 20) // math.isqrt(grade ** slope) + 1 for grade in range(2, number_of + 1)]
    rest, holding = total - most - (number_of - 1), [1] * (number_of - 1)
    while rest > 0:
        candidates = [i for i in range(number_of - 1) if holding[i] < most]
        pool, left = sum([portions[i] for i in candidates]), rest
        for i in candidates:
            extra = min(most - holding[i], max(1, left * portions[i] // pool), rest)
            holding[i] = holding[i] + extra
            rest = rest - extra
    return np.array([most] + holding)


def uneven(rng, number_of, total, reach, skew):
    if number_of == 2:
        one = jax.random.randint(rng, (), max(1, total - reach), min(reach, total - 1) + 1)
        return jnp.stack([one, total - one])
    lengths = jnp.asarray(split_up(number_of, total, reach, skew), jnp.int32)
    twos = (number_of - 1) // 2
    giver, taker = lengths[1:1 + 2 * twos:2], lengths[2:2 + 2 * twos:2]
    margin = jnp.minimum(giver - 1, reach - taker)
    shifted = jax.random.randint(jax.random.fold_in(rng, 1), (twos,), 0, 1 << 20) % (margin + 1)
    lengths = lengths.at[1:1 + 2 * twos:2].set(giver - shifted).at[2:2 + 2 * twos:2].set(taker + shifted)
    return lengths[jax.random.permutation(jax.random.fold_in(rng, 2), number_of)]


def normal_values(stream_key, extent, spread, bound, pieces=(), kind=jnp.bfloat16):
    entries = spread * jax.random.normal(stream_key, extent, jnp.float32)
    if pieces:
        entries = entries * shard_levels(stream_key, extent, pieces, -0.22, 0.18)
    return jnp.clip(entries, -bound, bound).astype(kind)


def setup_inputs(seed: int = 0) -> dict:
    arg_keys = jax.random.split(jax.random.key(seed), 7)
    return {
        "queries": draw_queries(jax.random.fold_in(arg_keys[6], 71), 0),
        "keys": draw_keys(jax.random.fold_in(arg_keys[6], 71), 0),
        "values": normal_values(arg_keys[2], (TOKEN_SLOTS, KEY_VALUE_HEADS * HEAD_SIZE), 1.0, 6.0, ((0, 32),)),
        "output_gradient": normal_values(arg_keys[3], (TOKEN_SLOTS, QUERY_HEADS * HEAD_SIZE), 1.0, 6.0, ((0, 32),)),
        "doc_blocks": uneven(arg_keys[4], DOCS, BLOCK_TOTAL, MOST_DOC_BLOCKS, 1).astype(jnp.int32),
        "doc_pad": with_ends(jax.random.randint(arg_keys[5], (DOCS,), 0, DEVICE_TOKENS), jax.random.fold_in(arg_keys[5], 1), 0, DEVICE_TOKENS - 1).astype(jnp.int32),
    }


def rounded(tensor):
    return lax.optimization_barrier(tensor.astype(jnp.bfloat16)).astype(jnp.float32)

def block_meta(block_ids, starts, doc_sizes, doc_pads, token_rows, block_count):
    in_range = (block_ids >= 0) & (block_ids < block_count)
    doc_index = lax.optimization_barrier(jnp.sum((starts[None, :] <= block_ids[:, None]).astype(jnp.int32), axis=1)) - 1
    doc_index = jnp.where(in_range, doc_index, -1)
    one_hot = jnp.arange(starts.shape[0], dtype=jnp.int32)[None, :] == doc_index[:, None]
    doc_ends = lax.optimization_barrier(jnp.sum(jnp.where(one_hot, (starts + doc_sizes)[None, :] * token_rows - doc_pads[None, :], 0), axis=1))
    positions = block_ids[:, None] * token_rows + jnp.arange(token_rows, dtype=jnp.int32)[None, :]
    is_valid = (positions < doc_ends[:, None]) & in_range[:, None]
    doc_ids = jnp.broadcast_to(doc_index[:, None], positions.shape)
    return (doc_ids.reshape(-1), positions.reshape(-1), is_valid.reshape(-1))

def allowed_pairs(query_info, key_info):
    same_doc = query_info[0][:, None] == key_info[0][None, :]
    causal = key_info[1][None, :] <= query_info[1][:, None]
    return same_doc & causal & query_info[2][:, None] & key_info[2][None, :]

def scores_of(query_rows, key_rows, score_scale):
    return jnp.einsum('tkgd,skd->kgts', query_rows.astype(jnp.float32), key_rows.astype(jnp.float32)) * score_scale

def softmax_parts(score_f32, pair_mask, query_valid):
    masked = jnp.where(pair_mask, score_f32, -jnp.inf)
    row_peak = jnp.where(query_valid, lax.optimization_barrier(jnp.max(masked, axis=-1)), 0.0)
    row_total = lax.optimization_barrier(jnp.sum(jnp.where(pair_mask, jnp.exp(score_f32 - row_peak[..., None]), 0.0), axis=-1))
    log_total = row_peak + jnp.log(jnp.where(query_valid, row_total, 1.0))
    weight = jnp.where(pair_mask, jnp.exp(score_f32 - log_total[..., None]), 0.0)
    return (log_total, weight)

def reference(queries, keys, values, output_gradient, doc_blocks, doc_pad):
    head_group_width = QUERY_HEADS // KEY_VALUE_HEADS
    score_scale = HEAD_SIZE ** (-0.5)
    backward_distance = MOST_DOC_BLOCKS - 1
    starts = jnp.cumsum(doc_blocks) - doc_blocks
    blocked_queries = queries.reshape(BLOCK_TOTAL, DEVICE_TOKENS, KEY_VALUE_HEADS, head_group_width, HEAD_SIZE)
    gradient_blocks = output_gradient.reshape(BLOCK_TOTAL, DEVICE_TOKENS, KEY_VALUE_HEADS, head_group_width, HEAD_SIZE)
    blocked_keys = keys.reshape(BLOCK_TOTAL, DEVICE_TOKENS, KEY_VALUE_HEADS, HEAD_SIZE)
    blocked_values = values.reshape(BLOCK_TOTAL, DEVICE_TOKENS, KEY_VALUE_HEADS, HEAD_SIZE)
    empty_key_values = jnp.zeros((backward_distance, DEVICE_TOKENS, KEY_VALUE_HEADS, HEAD_SIZE), keys.dtype)
    padded_keys = jnp.concatenate([empty_key_values, blocked_keys], axis=0)
    padded_values = jnp.concatenate([empty_key_values, blocked_values], axis=0)
    single = jnp.zeros((1,), jnp.int32)
    span = jnp.arange(MOST_DOC_BLOCKS, dtype=jnp.int32)

    def meta(block_ids):
        return block_meta(block_ids, starts, doc_blocks, doc_pad, DEVICE_TOKENS, BLOCK_TOTAL)

    def near_of(current_block_index):
        neighbor_keys = lax.dynamic_slice_in_dim(padded_keys, current_block_index, MOST_DOC_BLOCKS, 0).reshape(MOST_DOC_BLOCKS * DEVICE_TOKENS, KEY_VALUE_HEADS, HEAD_SIZE)
        neighbor_values = lax.dynamic_slice_in_dim(padded_values, current_block_index, MOST_DOC_BLOCKS, 0).reshape(MOST_DOC_BLOCKS * DEVICE_TOKENS, KEY_VALUE_HEADS, HEAD_SIZE)
        query_info = meta(current_block_index + single)
        pair_mask = allowed_pairs(query_info, meta(current_block_index - backward_distance + span))
        return (neighbor_keys, neighbor_values, pair_mask, query_info[2])

    def forward_one(current_block_index):
        neighbor_keys, neighbor_values, pair_mask, query_valid = near_of(current_block_index)
        score_f32 = scores_of(blocked_queries[current_block_index], neighbor_keys, score_scale)
        log_total, weight = softmax_parts(score_f32, pair_mask, query_valid)
        attn = jnp.einsum('kgts,skd->tkgd', rounded(weight), neighbor_values.astype(jnp.float32))
        return (attn.astype(jnp.bfloat16), log_total)
    attention_result, lse_all = lax.map(forward_one, jnp.arange(BLOCK_TOTAL, dtype=jnp.int32))
    delta_all = jnp.einsum('ntkgd,ntkgd->nkgt', gradient_blocks.astype(jnp.float32), attention_result.astype(jnp.float32))

    def query_grad(current_block_index):
        neighbor_keys, neighbor_values, pair_mask, query_valid = near_of(current_block_index)
        score_f32 = scores_of(blocked_queries[current_block_index], neighbor_keys, score_scale)
        weight = jnp.where(pair_mask, jnp.exp(score_f32 - lse_all[current_block_index][..., None]), 0.0)
        dprob = jnp.einsum('tkgd,skd->kgts', gradient_blocks[current_block_index].astype(jnp.float32), neighbor_values.astype(jnp.float32))
        dscore = rounded(weight * (dprob - delta_all[current_block_index][..., None]))
        grad_q = jnp.einsum('kgts,skd->tkgd', dscore, neighbor_keys.astype(jnp.float32)) * score_scale
        return grad_q.astype(jnp.bfloat16)
    full_query_gradient = lax.map(query_grad, jnp.arange(BLOCK_TOTAL, dtype=jnp.int32))
    empty_queries = jnp.zeros((backward_distance, DEVICE_TOKENS, KEY_VALUE_HEADS, head_group_width, HEAD_SIZE), queries.dtype)
    padded_queries = jnp.concatenate([blocked_queries, empty_queries], axis=0)
    padded_gradients = jnp.concatenate([gradient_blocks, empty_queries], axis=0)
    empty_statistics = jnp.zeros((backward_distance, KEY_VALUE_HEADS, head_group_width, DEVICE_TOKENS), jnp.float32)
    padded_log_sum = jnp.concatenate([lse_all, empty_statistics], axis=0)
    padded_delta_rows = jnp.concatenate([delta_all, empty_statistics], axis=0)

    def key_grad(current_block_index):
        following_queries = lax.dynamic_slice_in_dim(padded_queries, current_block_index, MOST_DOC_BLOCKS, 0).reshape(MOST_DOC_BLOCKS * DEVICE_TOKENS, KEY_VALUE_HEADS, head_group_width, HEAD_SIZE)
        following_gradients = lax.dynamic_slice_in_dim(padded_gradients, current_block_index, MOST_DOC_BLOCKS, 0).reshape(MOST_DOC_BLOCKS * DEVICE_TOKENS, KEY_VALUE_HEADS, head_group_width, HEAD_SIZE)
        following_log_sum = lax.dynamic_slice_in_dim(padded_log_sum, current_block_index, MOST_DOC_BLOCKS, 0).transpose(1, 2, 0, 3).reshape(KEY_VALUE_HEADS, head_group_width, MOST_DOC_BLOCKS * DEVICE_TOKENS)
        following_delta = lax.dynamic_slice_in_dim(padded_delta_rows, current_block_index, MOST_DOC_BLOCKS, 0).transpose(1, 2, 0, 3).reshape(KEY_VALUE_HEADS, head_group_width, MOST_DOC_BLOCKS * DEVICE_TOKENS)
        pair_mask = allowed_pairs(meta(current_block_index + span), meta(current_block_index + single))
        score_f32 = scores_of(following_queries, blocked_keys[current_block_index], score_scale)
        weight = jnp.where(pair_mask, jnp.exp(score_f32 - following_log_sum[..., None]), 0.0)
        dprob = jnp.einsum('tkgd,skd->kgts', following_gradients.astype(jnp.float32), blocked_values[current_block_index].astype(jnp.float32))
        dscore = rounded(weight * (dprob - following_delta[..., None]))
        grad_k = jnp.einsum('kgts,tkgd->skd', dscore, following_queries.astype(jnp.float32)) * score_scale
        grad_v = jnp.einsum('kgts,tkgd->skd', rounded(weight), following_gradients.astype(jnp.float32))
        return (grad_k.astype(jnp.bfloat16), grad_v.astype(jnp.bfloat16))
    full_key_gradient, full_value_gradient = lax.map(key_grad, jnp.arange(BLOCK_TOTAL, dtype=jnp.int32))
    return (attention_result.reshape(TOKEN_SLOTS, QUERY_HEADS * HEAD_SIZE), full_query_gradient.reshape(TOKEN_SLOTS, QUERY_HEADS * HEAD_SIZE), full_key_gradient.reshape(TOKEN_SLOTS, KEY_VALUE_HEADS * HEAD_SIZE), full_value_gradient.reshape(TOKEN_SLOTS, KEY_VALUE_HEADS * HEAD_SIZE))
```

```python
import functools
import jax
import jax.numpy as jnp
from jax import lax
from jax.experimental import pallas as pl
from jax.experimental.pallas import tpu as pltpu
from jax.sharding import PartitionSpec as P

QUERY_HEADS = 16
KEY_VALUE_HEADS = 4
HEAD_SIZE = 128
MOST_DOC_BLOCKS = 3
GROUP = QUERY_HEADS // KEY_VALUE_HEADS
AXES = ("dp", "ctx")
LOG2E = 1.4426950408889634
NEG = -1e30
CHUNKS = 2
LANE_HEADS = 2


def rotated(array, by):
    count = lax.axis_size(AXES)
    return lax.ppermute(array, AXES, [(i, (i + by) % count) for i in range(count)])


def doc_bounds(codes_ref, block, rows):
    def step(i, carry):
        start, first, end = carry
        code = codes_ref[i]
        size = code // rows
        mine = (start <= block) & (block < start + size)
        first = jnp.where(mine, start, first)
        end = jnp.where(mine, (start + size) * rows - code % rows, end)
        return start + size, first, end

    zero = jnp.int32(0)
    _, first, end = lax.fori_loop(0, codes_ref.shape[0], step, (zero, zero, zero))
    return first, end


def dot(a, b, contract):
    return lax.dot_general(
        a, b, ((contract[:1], contract[1:]), ((), ())), preferred_element_type=jnp.float32
    )


def attend(heads, codes_ref, q_ref, do_ref, k0_ref, v0_ref, r1_ref, r2_ref, *rest):
    attn_ref, dq_ref, own_ref, t1_ref, t2_ref = rest[-5:]
    rows = q_ref.shape[0]
    size = HEAD_SIZE
    block = lax.axis_index("dp") * lax.axis_size("ctx") + lax.axis_index("ctx")
    first, end = doc_bounds(codes_ref, block, rows)
    scale = HEAD_SIZE ** (-0.5)
    bias1 = jnp.where(first <= block - 1, 0.0, NEG).astype(jnp.float32)
    bias2 = jnp.where(first <= block - 2, 0.0, NEG).astype(jnp.float32)
    width = LANE_HEADS * rows
    key_at = lax.broadcasted_iota(jnp.int32, (rows, width), 0)
    query_at = lax.broadcasted_iota(jnp.int32, (rows, width), 1) % rows
    causal = jnp.where(key_at <= query_at, 0.0, NEG).astype(jnp.float32)
    lane = lax.broadcasted_iota(jnp.int32, (1, width), 1) % rows
    valid = block * rows + lane < end
    for head in range(heads):
        cols = slice(head * size, (head + 1) * size)
        key = jnp.concatenate(
            [r2_ref[:rows, cols], r1_ref[:rows, cols], k0_ref[:, cols]], axis=0
        )
        value = jnp.concatenate(
            [r2_ref[rows:, cols], r1_ref[rows:, cols], v0_ref[:, cols]], axis=0
        )
        dk = dv = None
        for part in range(GROUP // LANE_HEADS):
            names = [head * GROUP + part * LANE_HEADS + i for i in range(LANE_HEADS)]
            q = jnp.concatenate([q_ref[:, n * size : (n + 1) * size] for n in names], axis=0)
            do = jnp.concatenate([do_ref[:, n * size : (n + 1) * size] for n in names], axis=0)
            score = dot(key, q, (1, 1)) * (scale * LOG2E)
            s2 = score[:rows] + bias2
            s1 = score[rows : 2 * rows] + bias1
            s0 = score[2 * rows :] + causal
            peak = jnp.max(jnp.maximum(jnp.maximum(s2, s1), s0), axis=0, keepdims=True)
            e2, e1, e0 = jnp.exp2(s2 - peak), jnp.exp2(s1 - peak), jnp.exp2(s0 - peak)
            total = jnp.sum(e2 + e1 + e0, axis=0, keepdims=True)
            inverse = jnp.where(valid, 1.0 / total, 0.0)
            weight = jnp.concatenate([e2, e1, e0], axis=0) * inverse
            dprob = dot(value, do, (1, 1))
            delta = jnp.sum(weight * dprob, axis=0, keepdims=True)
            dscore = (weight * (dprob - delta)).astype(jnp.bfloat16)
            weight = weight.astype(jnp.bfloat16)
            out = dot(value, weight, (0, 0))
            dq = dot(key, dscore, (0, 0)) * scale
            for i, n in enumerate(names):
                at = slice(n * size, (n + 1) * size)
                lanes = slice(i * rows, (i + 1) * rows)
                attn_ref[:, at] = out[:, lanes].T.astype(jnp.bfloat16)
                dq_ref[:, at] = dq[:, lanes].T.astype(jnp.bfloat16)
            dv_part = dot(weight, do, (1, 0))
            dk_part = dot(dscore, q, (1, 0))
            dv = dv_part if dv is None else dv + dv_part
            dk = dk_part if dk is None else dk + dk_part
        dk = dk * scale
        t2_ref[:rows, cols] = dk[:rows].astype(jnp.bfloat16)
        t2_ref[rows:, cols] = dv[:rows].astype(jnp.bfloat16)
        t1_ref[:rows, cols] = dk[rows : 2 * rows].astype(jnp.bfloat16)
        t1_ref[rows:, cols] = dv[rows : 2 * rows].astype(jnp.bfloat16)
        own_ref[:rows, cols] = dk[2 * rows :]
        own_ref[rows:, cols] = dv[2 * rows :]


def call_attend(chunk, codes, q, do, keys, values, r1, r2, before):
    rows, q_width = q.shape
    heads = KEY_VALUE_HEADS // CHUNKS
    wide = heads * GROUP * HEAD_SIZE
    narrow = heads * HEAD_SIZE
    vmem = pltpu.VMEM
    q_spec = pl.BlockSpec((rows, wide), lambda i: (0, chunk), memory_space=vmem)
    kv_spec = pl.BlockSpec((rows, narrow), lambda i: (0, chunk), memory_space=vmem)
    whole = pl.BlockSpec((2 * rows, narrow), lambda i: (0, 0), memory_space=vmem)
    any_spec = pl.BlockSpec(memory_space=pl.ANY)
    bf16 = jnp.bfloat16
    shape = jax.ShapeDtypeStruct
    return pl.pallas_call(
        functools.partial(attend, heads),
        grid=(1,),
        name=f"attend{chunk}",
        in_specs=[pl.BlockSpec(memory_space=pltpu.SMEM), q_spec, q_spec, kv_spec, kv_spec]
        + [whole, whole]
        + [any_spec] * len(before),
        out_specs=[q_spec, q_spec, whole, whole, whole],
        out_shape=[
            shape((rows, q_width), bf16),
            shape((rows, q_width), bf16),
            shape((2 * rows, narrow), jnp.float32),
            shape((2 * rows, narrow), bf16),
            shape((2 * rows, narrow), bf16),
        ],
        input_output_aliases={7 + i: i for i in range(len(before))},
        cost_estimate=pl.CostEstimate(
            flops=12 * rows * 3 * rows * wide, bytes_accessed=8 * rows * wide, transcendentals=0
        ),
    )(codes, q, do, keys, values, r1, r2, *before)


def finish(chunks, *refs):
    dk_ref, dv_ref = refs[-2:]
    rows = dk_ref.shape[0]
    for c in range(chunks):
        own, r1, r2 = refs[3 * c : 3 * c + 3]
        width = own.shape[1]
        total = own[...] + r1[...].astype(jnp.float32) + r2[...].astype(jnp.float32)
        dk_ref[:, c * width : (c + 1) * width] = total[:rows].astype(jnp.bfloat16)
        dv_ref[:, c * width : (c + 1) * width] = total[rows:].astype(jnp.bfloat16)


def on_device(queries, keys, values, output_gradient, doc_blocks, doc_pad):
    rows = queries.shape[0]
    width = KEY_VALUE_HEADS * HEAD_SIZE // CHUNKS
    per = doc_blocks.shape[0]
    parts = lax.axis_size("dp")
    code = doc_blocks * rows + doc_pad
    spread = jnp.tile(code, parts)
    owner = jnp.arange(per * parts, dtype=jnp.int32) // per
    codes = lax.psum(jnp.where(owner == lax.axis_index("dp"), spread, 0), "dp")
    payloads = [
        jnp.concatenate(
            [keys[:, c * width : (c + 1) * width], values[:, c * width : (c + 1) * width]], axis=0
        )
        for c in range(CHUNKS)
    ]
    arrived = [(rotated(p, 1), rotated(p, 2)) for p in payloads]
    before = ()
    gathered = []
    for c in range(CHUNKS):
        r1, r2 = arrived[c]
        attn, dq, own, t1, t2 = call_attend(
            c, codes, queries, output_gradient, keys, values, r1, r2, before
        )
        before = (attn, dq)
        gathered += [own, rotated(t1, -1), rotated(t2, -2)]
    dk, dv = pl.pallas_call(
        functools.partial(finish, CHUNKS),
        name="finish",
        out_shape=[jax.ShapeDtypeStruct(keys.shape, jnp.bfloat16)] * 2,
    )(*gathered)
    return attn, dq, dk, dv


def solution(mesh):
    rows = P(("dp", "ctx"), None)
    return jax.shard_map(
        on_device,
        mesh=mesh,
        in_specs=(rows, rows, rows, rows, P("dp"), P("dp")),
        out_specs=(rows, rows, rows, rows),
        check_vma=False,
    )
```

```python
import functools
import jax
import jax.numpy as jnp
from jax import lax
from jax.experimental import pallas as pl
from jax.experimental.pallas import tpu as pltpu
from jax.sharding import PartitionSpec as P

QUERY_HEADS = 16
KEY_VALUE_HEADS = 4
HEAD_SIZE = 128
GROUP = QUERY_HEADS // KEY_VALUE_HEADS
AXES = ("dp", "ctx")
LOG2E = 1.4426950408889634
NEG = -1e30
CHUNKS = 2
LANE_HEADS = 2


def rotated(array, by):
    count = lax.axis_size(AXES)
    return lax.ppermute(array, AXES, [(i, (i + by) % count) for i in range(count)])


def doc_bounds(info_ref, block, rows):
    docs = info_ref.shape[0] // 2

    def step(i, carry):
        start, first, end = carry
        after = start + info_ref[i]
        mine = (start <= block) & (block < after)
        first = jnp.where(mine, start, first)
        end = jnp.where(mine, after * rows - info_ref[docs + i], end)
        return after, first, end

    zero = jnp.int32(0)
    _, first, end = lax.fori_loop(0, docs, step, (zero, zero, zero), unroll=min(docs, 16))
    return first, end


def dot(a, b, contract):
    return lax.dot_general(
        a, b, ((contract[:1], contract[1:]), ((), ())), preferred_element_type=jnp.float32
    )


def attend(chunk, heads, info_ref, q_ref, do_ref, k0_ref, v0_ref, r1_ref, r2_ref, *rest):
    attn_ref, dq_ref, own_ref, t1_ref, t2_ref = rest[-5:]
    rows = q_ref.shape[0]
    size = HEAD_SIZE
    block = lax.axis_index("dp") * lax.axis_size("ctx") + lax.axis_index("ctx")
    first, end = doc_bounds(info_ref, block, rows)
    scale = HEAD_SIZE ** (-0.5)
    bias1 = jnp.where(first <= block - 1, 0.0, NEG).astype(jnp.float32)
    bias2 = jnp.where(first <= block - 2, 0.0, NEG).astype(jnp.float32)
    width = LANE_HEADS * rows
    key_at = lax.broadcasted_iota(jnp.int32, (rows, width), 0)
    query_at = lax.broadcasted_iota(jnp.int32, (rows, width), 1) % rows
    causal = jnp.where(key_at <= query_at, 0.0, NEG).astype(jnp.float32)
    lane = lax.broadcasted_iota(jnp.int32, (1, width), 1) % rows
    valid = block * rows + lane < end
    parts = GROUP // LANE_HEADS
    units = [(head, part) for head in range(heads) for part in range(parts)]

    def of_head(head):
        cols = slice(head * size, (head + 1) * size)
        mine = slice((chunk * heads + head) * size, (chunk * heads + head + 1) * size)
        key = jnp.concatenate([r2_ref[:rows, cols], r1_ref[:rows, cols], k0_ref[:, mine]], axis=0)
        value = jnp.concatenate([r2_ref[rows:, cols], r1_ref[rows:, cols], v0_ref[:, mine]], axis=0)
        return key, value

    def names_of(unit):
        head, part = unit
        start = (chunk * heads + head) * GROUP + part * LANE_HEADS
        return range(start, start + LANE_HEADS)

    def stacked(ref, unit):
        return jnp.concatenate([ref[:, n * size : (n + 1) * size] for n in names_of(unit)], axis=0)

    def products(unit):
        key, value = of_head(unit[0])
        return dot(key, stacked(q_ref, unit), (1, 1)), dot(value, stacked(do_ref, unit), (1, 1))

    def weights(score, dprob):
        score = score * (scale * LOG2E)
        s2 = score[:rows] + bias2
        s1 = score[rows : 2 * rows] + bias1
        s0 = score[2 * rows :] + causal
        peak = jnp.max(jnp.maximum(jnp.maximum(s2, s1), s0), axis=0, keepdims=True)
        e2, e1, e0 = jnp.exp2(s2 - peak), jnp.exp2(s1 - peak), jnp.exp2(s0 - peak)
        total = jnp.sum(e2 + e1 + e0, axis=0, keepdims=True)
        inverse = jnp.where(valid, 1.0 / total, 0.0)
        weight = jnp.concatenate([e2, e1, e0], axis=0) * inverse
        delta = jnp.sum(weight * dprob, axis=0, keepdims=True)
        dscore = (weight * (dprob - delta)).astype(jnp.bfloat16)
        return weight.astype(jnp.bfloat16), dscore

    sums = {}

    def outputs(unit, weight, dscore):
        head, part = unit
        key, value = of_head(head)
        out = dot(value, weight, (0, 0))
        dq = dot(key, dscore, (0, 0)) * scale
        for i, n in enumerate(names_of(unit)):
            at = slice(n * size, (n + 1) * size)
            lanes = slice(i * rows, (i + 1) * rows)
            attn_ref[:, at] = out[:, lanes].T.astype(jnp.bfloat16)
            dq_ref[:, at] = dq[:, lanes].T.astype(jnp.bfloat16)
        dv = dot(weight, stacked(do_ref, unit), (1, 0))
        dk = dot(dscore, stacked(q_ref, unit), (1, 0)) * scale
        if part:
            dk, dv = sums[head][0] + dk, sums[head][1] + dv
        sums[head] = dk, dv
        if part < parts - 1:
            return
        cols = slice(head * size, (head + 1) * size)
        t2_ref[:rows, cols] = dk[:rows].astype(jnp.bfloat16)
        t2_ref[rows:, cols] = dv[:rows].astype(jnp.bfloat16)
        t1_ref[:rows, cols] = dk[rows : 2 * rows].astype(jnp.bfloat16)
        t1_ref[rows:, cols] = dv[rows : 2 * rows].astype(jnp.bfloat16)
        own_ref[:rows, cols] = dk[2 * rows :]
        own_ref[rows:, cols] = dv[2 * rows :]

    ready = products(units[0])
    for i, unit in enumerate(units):
        upcoming = products(units[i + 1]) if i + 1 < len(units) else None
        outputs(unit, *weights(*ready))
        ready = upcoming


def placed(array):
    return pltpu.with_memory_space_constraint(array, pltpu.VMEM)


def call_attend(chunk, info, q, do, keys, values, r1, r2, before):
    rows, q_width = q.shape
    heads = KEY_VALUE_HEADS // CHUNKS
    wide = heads * GROUP * HEAD_SIZE
    narrow = heads * HEAD_SIZE
    bf16 = jnp.bfloat16
    vmem = pl.BlockSpec(memory_space=pltpu.VMEM)
    return pl.pallas_call(
        functools.partial(attend, chunk, heads),
        in_specs=[pl.BlockSpec(memory_space=pltpu.SMEM)] + [vmem] * 6 + [vmem] * len(before),
        out_specs=[vmem] * 5,
        out_shape=[
            pltpu.VMEM((rows, q_width), bf16),
            pltpu.VMEM((rows, q_width), bf16),
            pltpu.VMEM((2 * rows, narrow), jnp.float32),
            pltpu.VMEM((2 * rows, narrow), bf16),
            pltpu.VMEM((2 * rows, narrow), bf16),
        ],
        input_output_aliases={7 + i: i for i in range(len(before))},
        compiler_params=pltpu.CompilerParams(vmem_limit_bytes=20 << 20),
        cost_estimate=pl.CostEstimate(
            flops=12 * rows * 3 * rows * wide, bytes_accessed=8 * rows * wide, transcendentals=0
        ),
    )(info, *map(placed, (q, do, keys, values, r1, r2, *before)))


def finish(chunks, *refs):
    dk_ref, dv_ref = refs[-2:]
    rows = dk_ref.shape[0]
    for c in range(chunks):
        own, r1, r2 = refs[3 * c : 3 * c + 3]
        width = own.shape[1]
        total = own[...] + r1[...].astype(jnp.float32) + r2[...].astype(jnp.float32)
        dk_ref[:, c * width : (c + 1) * width] = total[:rows].astype(jnp.bfloat16)
        dv_ref[:, c * width : (c + 1) * width] = total[rows:].astype(jnp.bfloat16)


def body(queries, keys, values, output_gradient, doc_blocks, doc_pad):
    width = KEY_VALUE_HEADS * HEAD_SIZE // CHUNKS
    per = doc_blocks.shape[0]
    parts = lax.axis_size("dp")
    mine = jnp.arange(parts, dtype=jnp.int32)[:, None] == lax.axis_index("dp")
    info = jnp.concatenate(
        [jnp.where(mine, part[None, :], 0).reshape(per * parts) for part in (doc_blocks, doc_pad)]
    )
    info = lax.psum(info, "dp")
    payloads = [
        jnp.concatenate(
            [keys[:, c * width : (c + 1) * width], values[:, c * width : (c + 1) * width]], axis=0
        )
        for c in range(CHUNKS)
    ]
    arrived = []
    for p in payloads:
        near = rotated(p, 1)
        far = rotated(p, 2)
        arrived.append((near, far))
    before = ()
    gathered = []
    for c in range(CHUNKS):
        r1, r2 = arrived[c]
        attn, dq, own, t1, t2 = call_attend(
            c, info, queries, output_gradient, keys, values, r1, r2, before
        )
        before = (attn, dq)
        gathered += [own, rotated(t1, -1), rotated(t2, -2)]
    dk, dv = pl.pallas_call(
        functools.partial(finish, CHUNKS),
        name="finish",
        compiler_params=pltpu.CompilerParams(vmem_limit_bytes=20 << 20),
        out_shape=[jax.ShapeDtypeStruct(keys.shape, jnp.bfloat16)] * 2,
    )(*map(placed, gathered))
    return attn, dq, dk, dv


def solution(mesh):
    rows = P(("dp", "ctx"), None)
    return jax.shard_map(
        body,
        mesh=mesh,
        in_specs=(rows, rows, rows, rows, P("dp"), P("dp")),
        out_specs=(rows, rows, rows, rows),
        check_vma=False,
    )
```
